32 devices in a mesh: srow: 8 (over y, x, core), scol: 4 (over z).
Axes of the slice: x: 2, y: 2, z: 4, core: 2. Of those that a mesh axis runs over, the one named last changes fastest.
Arguments:
- factor_state: float32 [8, 512, 2, 4, 512], P('srow', None, None, 'scol'), may hold values from -40 to 40, as said below
- data: float32 [8, 512, 4096], P('srow', None, 'scol'), may hold values from -6 to 6
Outputs:
- factor_out: float32 [8, 512, 2, 4, 512], P('srow', None, None, 'scol')
- data_out: float32 [8, 512, 4096], P('srow', None, 'scol')
The draws below stay inside these ranges and needn't reach their ends.
Inputs may be any that keep to these rules, and one draw needn't show every extreme that they name: factor_state is exactly symmetric and positive definite as the matrix A.
All inputs are finite; a program needn't handle non-finite values.
Results may differ from the reference program's by a relative error of at most 0.00005.
Values sent between devices are 32-bit elements; how exact they have to be, the bound alone decides.
No kernel may reach another device: no remote copies, remote signals or barrier semaphores. Data moves between devices by JAX's collectives and lax.ppermute only.
A program may use at most 128 MiB of HBM per device.

```python
import jax
import jax.numpy as jnp
from jax import lax

B = 512
TILES = 8
CYCLE = 4
GROUPS = 2
TIME = 4096


def draw_factor_state(key, part):
    site_count = TILES * B
    latent_rank = 2 * B
    key_latent = jax.random.fold_in(key, 11)
    key_nugget = jax.random.fold_in(key, 12)
    latent = jax.random.normal(key_latent, (site_count, latent_rank), jnp.float32)
    gram_matrix = jnp.dot(latent, latent.T, precision=lax.Precision.HIGHEST) / latent_rank
    nugget = jax.random.uniform(key_nugget, (site_count,), jnp.float32, 0.3, 1.0)
    whole_matrix = gram_matrix + jnp.diag(nugget)
    whole_matrix = 0.5 * (whole_matrix + whole_matrix.T)
    return whole_matrix.reshape(TILES, B, GROUPS, CYCLE, B)


def shard_levels(stream_key, shape, shards, smallest, top_value):
    def one(axis_at, blocks):
        steps = jax.random.uniform(jax.random.fold_in(jax.random.fold_in(stream_key, 6), axis_at), (blocks,), jnp.float32, smallest / len(shards), top_value / len(shards))
        return jnp.repeat(jnp.exp(steps), shape[axis_at] // blocks).reshape((-1,) + (1,) * (len(shape) - axis_at - 1))

    loudness = one(*shards[0])
    for cut in shards[1:]:
        loudness = loudness * one(*cut)
    return loudness


def normal_values(key, dims, width, most, pieces=(), kind=jnp.bfloat16):
    loudness = shard_levels(key, dims, pieces, -0.22, 0.18) if pieces else 1.0
    array = jax.random.normal(key, dims, jnp.float32) * width * loudness
    return jnp.minimum(jnp.maximum(array, -most), most).astype(kind)


def setup_inputs(seed: int = 0) -> dict:
    streams_of = jax.random.split(jax.random.key(seed), 3)
    factor_state = draw_factor_state(jax.random.fold_in(streams_of[2], 71), 0)
    data = normal_values(streams_of[1], (TILES, B, TIME), 1.0, 6.0, ((0, 8), (2, 4)), jnp.float32)
    return {"factor_state": factor_state, "data": data}


def reference(factor_state, data):
    site_count = TILES * B
    highest = lax.Precision.HIGHEST
    whole_matrix = factor_state.reshape(site_count, site_count)
    lower_tile = jnp.linalg.cholesky(whole_matrix[:B, :B])
    panel_tiles = jax.scipy.linalg.solve_triangular(lower_tile, whole_matrix[B:, :B].T, lower=True).T
    trailing = whole_matrix[B:, B:] - jnp.dot(panel_tiles, panel_tiles.T, precision=highest)
    first_rows = jnp.concatenate([lower_tile, jnp.zeros((B, site_count - B), jnp.float32)], axis=1)
    later_rows = jnp.concatenate([panel_tiles, trailing], axis=1)
    factor_out = jnp.concatenate([first_rows, later_rows], axis=0).reshape(TILES, B, GROUPS, CYCLE, B)
    data_matrix = data.reshape(site_count, TIME)
    solved = jax.scipy.linalg.solve_triangular(lower_tile, data_matrix[:B], lower=True)
    remain = data_matrix[B:] - jnp.dot(panel_tiles, solved, precision=highest)
    data_out = jnp.concatenate([solved, remain], axis=0).reshape(TILES, B, TIME)
    return (factor_out, data_out)
```

```python
import jax
import jax.numpy as jnp
from jax import lax
from jax.experimental import pallas as pl
from jax.experimental.pallas import tpu as pltpu
from jax.sharding import PartitionSpec as P

HIGHEST = lax.Precision.HIGHEST
F32 = jnp.float32
BF16 = jnp.bfloat16
VMEM = pl.BlockSpec(memory_space=pltpu.VMEM)
AXES = ("srow", "scol")


def lane_splat(x, lane):
    return jnp.broadcast_to(x[:, lane : lane + 1], (8, 128))


def row_splat(x, row):
    return jnp.broadcast_to(x[row : row + 1, :], (8, 128))


def total(terms):
    terms = list(terms)
    while len(terms) > 1:
        pairs = [terms[i] + terms[i + 1] for i in range(0, len(terms) - 1, 2)]
        terms = pairs + terms[2 * len(pairs) :]
    return terms[0]


def gather_rows(rows):
    sub = lax.broadcasted_iota(jnp.int32, (8, 128), 0)
    out = rows[0]
    for a in range(1, 8):
        out = jnp.where(sub == a, rows[a], out)
    return out


def factor_block(m_ref, u_ref, v_ref):
    lane = lax.broadcasted_iota(jnp.int32, (8, 128), 1)
    sub = lax.broadcasted_iota(jnp.int32, (8, 128), 0)
    count = 16
    left = [m_ref[8 * i : 8 * i + 8, :] for i in range(count)]
    right = [(lane == sub + 8 * i).astype(F32) for i in range(count)]
    for k in range(count):
        x, y = left[k], right[k]
        cols = [lane_splat(x, 8 * k + b) for b in range(8)]
        g = {(a, b): row_splat(cols[b], a) for a in range(8) for b in range(a + 1)}
        t, r = {}, []
        for j in range(8):
            r.append(1.0 / g[j, j])
            m = {a: g[a, j] * r[j] for a in range(j + 1, 8)}
            for a in range(j + 1, 8):
                for b in range(j + 1, a + 1):
                    g[a, b] = g[a, b] - m[a] * g[b, j]
                for c in range(j):
                    t[a, c] = t[a, c] - m[a] * t[j, c]
                t[a, j] = -m[a]
        s = [lax.rsqrt(g[j, j]) for j in range(8)]

        def forward(rows):
            return [total([rows[a]] + [t[a, b] * rows[b] for b in range(a)]) for a in range(8)]

        def backward(rows):
            w = [rows[a] * r[a] for a in range(8)]
            return [total([w[b]] + [t[a, b] * w[a] for a in range(b + 1, 8)]) for b in range(8)]

        u = forward([row_splat(x, a) for a in range(8)])
        v = forward([row_splat(y, a) for a in range(8)])
        scaled = gather_rows([u[a] * s[a] for a in range(8)])
        u_ref[8 * k : 8 * k + 8, :] = jnp.where(lane >= sub + 8 * k, scaled, 0.0)
        v_ref[8 * k : 8 * k + 8, :] = gather_rows([v[a] * s[a] for a in range(8)])
        if k < count - 1:
            zu, zv = backward(u), backward(v)
            for i in range(k + 1, count):
                q = [lane_splat(left[i], 8 * k + b) for b in range(8)]
                left[i] = left[i] - total([q[b] * zu[b] for b in range(8)])
                right[i] = right[i] - total([q[b] * zv[b] for b in range(8)])


def cholesky_kernel(t_ref, u_ref, inv_ref, w_ref, d_ref, v_ref, ud_ref):
    n = u_ref.shape[0]
    count = n // 128
    stride = t_ref.shape[0] // n

    @pl.when(jnp.logical_and(lax.axis_index("srow") == 0, lax.axis_index("scol") == 0))
    def _():
        for q in range(count):
            w_ref[:, q * 128 : q * 128 + 128] = t_ref[pl.ds(q, n, stride=stride), :]
        row = lax.broadcasted_iota(jnp.int32, (n, n), 0)
        col = lax.broadcasted_iota(jnp.int32, (n, n), 1)
        w_ref[:, n:] = (row == col).astype(F32)

        def step(k, c):
            o = pl.multiple_of(k * 128, 128)
            d_ref[...] = w_ref[pl.ds(o, 128), pl.ds(o, 128)]
            factor_block(d_ref, ud_ref, v_ref)
            new = jnp.dot(v_ref[...], w_ref[pl.ds(o, 128), :], precision=HIGHEST, preferred_element_type=F32)
            col = lax.broadcasted_iota(jnp.int32, (128, 2 * n), 1)
            new = jnp.where(col >= o + 128, new, 0.0)
            w_ref[pl.ds(o, 128), :] = new
            u_ref[pl.ds(o, 128), :] = new[:, :n]
            u_ref[pl.ds(o, 128), pl.ds(o, 128)] = ud_ref[...]
            inv_ref[pl.ds(o, 128), :] = new[:, n:]

            def inner(i, c):
                oi = pl.multiple_of(i * 128, 128)
                lhs = w_ref[pl.ds(o, 128), pl.ds(oi, 128)]
                w_ref[pl.ds(oi, 128), :] -= lax.dot_general(
                    lhs, w_ref[pl.ds(o, 128), :], (((0,), (0,)), ((), ())), precision=HIGHEST, preferred_element_type=F32
                )
                return c

            lax.fori_loop(k + 1, count, inner, 0)
            return c

        lax.fori_loop(0, count, step, 0)


def factor_corner(tiles, n):
    out = jax.ShapeDtypeStruct((n, n), F32)
    return pl.pallas_call(
        cholesky_kernel,
        out_shape=(out, out),
        in_specs=[VMEM],
        out_specs=(VMEM, VMEM),
        scratch_shapes=[pltpu.VMEM((n, 2 * n), F32)] + [pltpu.VMEM((128, 128), F32)] * 3,
        name="corner",
    )(tiles)


def split(x):
    high = x.astype(BF16)
    return high, (x - high.astype(F32)).astype(BF16)


def product(a, b, dims=((1,), (0,))):
    def dot(x, y):
        return lax.dot_general(x, y, (dims, ((), ())), preferred_element_type=F32)

    return dot(a[0], b[0]) + (dot(a[0], b[1]) + dot(a[1], b[0]))


def update_kernel(u_ref, inv_ref, first_ref, row_ref, lead_ref, own_ref, data_ref, fout_ref, dout_ref):
    n = inv_ref.shape[0]
    lanes = n // 128
    groups = own_ref.shape[0] // (n * lanes)
    top = lax.axis_index("srow") == 0
    front = lax.axis_index("scol") == 0
    inverse = split(inv_ref[...])
    first = jnp.concatenate([first_ref[pl.ds(q, n, stride=lanes), :] for q in range(lanes)], axis=1)
    panel = product(split(first), inverse, ((1,), (1,)))
    panel_parts = split(panel)

    def piece(ref, m, q):
        return ref.at[pl.ds(m * lanes + q, n, stride=groups * lanes), :]

    for m in range(groups):
        block = jnp.concatenate([piece(row_ref, m, q)[...] for q in range(lanes)], axis=1)
        solved = product(inverse, split(block))
        change = product(panel_parts, split(solved))
        for q in range(lanes):
            cut = slice(q * 128, q * 128 + 128)
            new = piece(own_ref, m, q)[...] - change[:, cut]
            low = 0.0
            if m == 0:
                new = jnp.where(front, panel[:, cut], new)
                low = jnp.where(front, u_ref[cut, :].T, 0.0)
            piece(fout_ref, m, q)[...] = jnp.where(top, low, new)
    for c in range(0, data_ref.shape[1], n):
        cut = slice(c, c + n)
        solved = product(inverse, split(lead_ref[:, cut]))
        change = product(panel_parts, split(solved))
        dout_ref[:, cut] = jnp.where(top, solved, data_ref[:, cut] - change)


def update(upper, inverse, first, row, lead, own, data):
    return pl.pallas_call(
        update_kernel,
        out_shape=(jax.ShapeDtypeStruct(own.shape, F32), jax.ShapeDtypeStruct(data.shape, F32)),
        in_specs=[VMEM] * 7,
        out_specs=(VMEM, VMEM),
        compiler_params=pltpu.CompilerParams(vmem_limit_bytes=56 << 20),
        name="update",
    )(upper, inverse, first, row, lead, own, data)


def powers(count):
    out, s = [], 1
    while s < count:
        out.append(s)
        s *= 2
    return out[::-1]


def broadcast(value, axis, strides):
    size, index = lax.axis_size(axis), lax.axis_index(axis)
    have = [0]
    for s in strides:
        pairs = [(h, h + s) for h in have if h + s < size]
        got = lax.ppermute(value, axis, pairs)
        takes = False
        for _, d in pairs:
            takes = jnp.logical_or(takes, index == d)
        value = jnp.where(takes, got, value)
        have += [d for _, d in pairs]
    return value


def per_device(factor_state, data):
    n, groups = factor_state.shape[1], factor_state.shape[2]
    rows, cols = lax.axis_size("srow"), lax.axis_size("scol")
    own = factor_state.reshape(n * groups * n // 128, 128)
    own_data = data[0]
    down = powers(rows)
    swapped = down[:-1][::-1] + down[-1:]
    first = factor_state[0, :, 0, 0, :].reshape(n * n // 128, 128)
    row = broadcast(own, "srow", down)
    lead = broadcast(own_data, "srow", swapped)
    first = broadcast(first, "scol", powers(cols))
    upper, inverse = factor_corner(own, n)
    inverse = broadcast(inverse, "scol", powers(cols))
    inverse = broadcast(inverse, "srow", down)
    factor_out, data_out = update(upper, inverse, first, row, lead, own, own_data)
    return factor_out.reshape(factor_state.shape), data_out[None]


def solution(mesh):
    return jax.shard_map(
        per_device,
        mesh=mesh,
        in_specs=(P("srow", None, None, "scol", None), P("srow", None, "scol")),
        out_specs=(P("srow", None, None, "scol", None), P("srow", None, "scol")),
        check_vma=False,
    )
```
